128 devices in a mesh: period: 8 (over x, y_hi), tile: 16 (over y_lo, z, core).
Axes of the slice: x: 4, y: 4 (y_hi: 2, y_lo: 2; y = y_hi * 2 + y_lo), z: 4, core: 2. Of those that a mesh axis runs over, the one named last changes fastest.
Arguments:
- block_inv: bfloat16 [8, 16384, 128], P('period', 'tile'), may hold values from -4 to 5, as said below
- linking: bfloat16 [8, 16384, 2048], P('period', 'tile'), may hold values from -0.046875 to 0.046875
- block_mask: int32 [8, 16], P('period'), may hold values 0 or 1
- period_rhs: float32 [8, 16384], P('period', 'tile'), may hold values from -6 to 6
- retention: float32 [8, 2048], P('period', 'tile'), may hold values from 0.2 to 1
- invest_cols: bfloat16 [8, 16384, 4096], P('period', 'tile'), may hold values from -1 to 1
- invest_diag: float32 [1024], replicated, may hold values from 0.5 to 2
Outputs:
- period_step: float32 [8, 16384], P('period', 'tile')
- boundary: float32 [8, 2048], P('period', 'tile')
- factor_top: float32 [1024, 1024], replicated
- factor_below: float32 [3072, 1024], P(('period', 'tile'))
The draws below stay inside these ranges and needn't reach their ends.
Inputs may be any that keep to these rules, and one draw needn't show every extreme that they name: `block_inv`: every 128 x 128 block is symmetric positive definite.
All inputs are finite; a program needn't handle non-finite values. No bound on the sum of `block_mask` on one device may be relied on, other than what follows from the above.
Results may differ from the reference program's by a relative error of at most 0.0029.
Values sent between devices are 32-bit elements; how exact they have to be, the bound alone decides.
No kernel may reach another device: no remote copies, remote signals or barrier semaphores. Data moves between devices by JAX's collectives and lax.ppermute only.
A program may use at most 128 MiB of HBM per device.

```python
import math
import jax
import jax.numpy as jnp
from jax import lax

HB = 128
SB = 128
NB = 2048
NI = 4096
NC = 1024
S = 8
R = 16384
NBLK = 16


def draw_block_inv(key, part):
    key_mix, key_diag = jax.random.split(jax.random.fold_in(key, 11))
    blocks = R // HB
    mixing = jnp.clip(jax.random.normal(key_mix, (S, blocks, HB, HB), jnp.float32), -4.0, 4.0)
    diagonal = jnp.exp(jax.random.uniform(key_diag, (S, blocks, HB), jnp.float32, math.log(0.5), 0.0))
    gram_part = jnp.einsum('sjab,sjcb->sjac', mixing, mixing) / (4.0 * HB)
    inverse = gram_part + diagonal[..., None] * jnp.eye(HB, dtype=jnp.float32)
    return inverse.reshape(S, R, HB).astype(jnp.bfloat16)


def draw_invest_cols(key, part):
    base_key = jax.random.fold_in(key, 23)
    key_choose, key_weight = jax.random.split(jax.random.fold_in(base_key, 1))
    factor_count = NI // 2
    chosen = jax.random.randint(key_choose, (NI, 4), 0, factor_count)
    weights = jnp.clip(0.5 * jax.random.normal(key_weight, (NI, 4), jnp.float32), -1.0, 1.0)
    spread_scale = (0.5 / (S * R)) ** 0.5

    def one_section(section):
        key_own, key_shared = jax.random.split(jax.random.fold_in(base_key, 100 + section))
        own_noise = jnp.clip(jax.random.normal(key_own, (R, NI), jnp.float32), -4.0, 4.0)
        shared_noise = jnp.clip(jax.random.normal(key_shared, (R, factor_count), jnp.float32), -4.0, 4.0)
        blended = own_noise
        for member in range(4):
            blended = blended + weights[:, member][None, :] * jnp.take(shared_noise, chosen[:, member], axis=1)
        return (spread_scale * blended).astype(jnp.bfloat16)
    return lax.map(one_section, jnp.arange(S, dtype=jnp.int32))


def plant(drawn, key, low, high):
    extent = drawn.shape
    spot = [jax.random.randint(jax.random.fold_in(key, axis), (), 0, extent[axis]) for axis in range(len(extent))]
    drawn = drawn.at[tuple(spot)].set(low)
    longest = extent.index(max(extent))
    spot[longest] = (spot[longest] + 1) % extent[longest]
    return drawn.at[tuple(spot)].set(high)


def shard_levels(stream_key, dims, pieces, least, largest):
    def one(position, shards_of):
        steps = jax.random.uniform(jax.random.fold_in(jax.random.fold_in(stream_key, 6), position), (shards_of,), jnp.float32, least / len(pieces), largest / len(pieces))
        return jnp.repeat(jnp.exp(steps), dims[position] // shards_of).reshape((-1,) + (1,) * (len(dims) - position - 1))

    gain = one(*pieces[0])
    for cut in pieces[1:]:
        gain = gain * one(*cut)
    return gain


def gaussian(own_key, dims, scale, limit, shards=(), held_as=jnp.bfloat16):
    result = scale * jax.random.normal(own_key, dims, jnp.float32)
    if shards:
        result = result * shard_levels(own_key, dims, shards, -0.22, 0.18)
    return jnp.clip(result, -limit, limit).astype(held_as)


def setup_inputs(seed: int = 0) -> dict:
    arg_keys = jax.random.split(jax.random.key(seed), 8)
    block_inv = draw_block_inv(jax.random.fold_in(arg_keys[7], 71), 0)
    linking = gaussian(arg_keys[1], (S, R, NB), R ** -0.5, 0.046875, ((0, 8), (1, 16)))
    block_mask = plant((jax.random.randint(arg_keys[2], (S, NBLK), 0, 4) < 3).astype(jnp.int32), jax.random.fold_in(arg_keys[2], 1), 0, 1)
    period_rhs = gaussian(arg_keys[3], (S, R), 1.0, 6.0, ((0, 8), (1, 16)), jnp.float32)
    retention = jnp.clip(jnp.exp(math.log(1.0) - 1.609438 * jax.random.uniform(arg_keys[4], (S, NB), jnp.float32) ** shard_levels(arg_keys[4], (S, NB), ((0, 8), (1, 16)), -0.2, 0.2)), 0.2, 1.0)
    invest_cols = draw_invest_cols(jax.random.fold_in(arg_keys[7], 71), 0)
    invest_diag = jnp.clip(jnp.exp(jax.random.uniform(arg_keys[6], (NC,), jnp.float32, math.log(0.5), math.log(2.0))), 0.5, 2.0)
    return {"block_inv": block_inv, "linking": linking, "block_mask": block_mask, "period_rhs": period_rhs, "retention": retention, "invest_cols": invest_cols, "invest_diag": invest_diag}


highest = lax.Precision.HIGHEST

def hourly(inverse, values):
    hour_rows = inverse.shape[1]
    blocks = inverse.shape[0] // hour_rows
    stacked = inverse.astype(jnp.float32).reshape(blocks, hour_rows, hour_rows)
    shaped = values.astype(jnp.float32).reshape(blocks, hour_rows, -1)
    return jnp.einsum('jab,jbn->jan', stacked, shaped, precision=highest).reshape(values.shape)

def reference(block_inv, linking, block_mask, period_rhs, retention, invest_cols, invest_diag):
    sections = block_inv.shape[0]
    spread = jnp.repeat(block_mask, SB, axis=1).astype(jnp.bfloat16)
    masked = linking * spread[:, None, :]

    def local_terms(packed):
        inverse, columns, rhs_row = packed
        solved_rhs = hourly(inverse, rhs_row)
        solved_half = solved_rhs.astype(jnp.bfloat16)
        solved_links = hourly(inverse, columns).astype(jnp.bfloat16)
        charge = jnp.dot(solved_half.astype(jnp.float32), columns.astype(jnp.float32), preferred_element_type=jnp.float32)
        schur_block = jnp.einsum('rkb,rkc->kbc', columns.astype(jnp.float32).reshape(R, NBLK, SB), solved_links.astype(jnp.float32).reshape(R, NBLK, SB), precision=highest)
        return (solved_rhs, charge, schur_block)
    solved_all, charge_all, schur_all = lax.map(local_terms, (block_inv, masked, period_rhs))

    def advance(carried, packed):
        charge, schur_block, keep_rate = packed
        updated = charge.reshape(NBLK, SB) + keep_rate.reshape(NBLK, SB) * jnp.einsum('kbc,kc->kb', schur_block, carried, precision=highest)
        return (updated, updated)
    zero_state = jnp.zeros((NBLK, SB), jnp.float32)
    final_state, states = lax.scan(advance, zero_state, (charge_all, schur_all, retention))
    boundary = states.reshape(sections, NB)
    following = jnp.concatenate([boundary[1:], jnp.zeros((1, NB), jnp.float32)], axis=0)
    change = (boundary - following).astype(jnp.bfloat16)

    def correction(packed):
        inverse, columns, solved_rhs, change_row = packed
        linked = jnp.dot(columns.astype(jnp.float32), change_row.astype(jnp.float32), preferred_element_type=jnp.float32)
        return solved_rhs - hourly(inverse, linked)
    period_step = lax.map(correction, (block_inv, masked, solved_all, change))

    def invest_term(running, packed):
        inverse, columns = packed
        scaled_cols = hourly(inverse, columns[:, :NC]).astype(jnp.bfloat16)
        return (running + jnp.dot(columns.T.astype(jnp.float32), scaled_cols.astype(jnp.float32), preferred_element_type=jnp.float32), None)
    initial = jnp.concatenate([jnp.diag(invest_diag), jnp.zeros((NI - NC, NC), jnp.float32)], axis=0)
    running, unused = lax.scan(invest_term, initial, (block_inv, invest_cols))
    factor_top = jnp.linalg.cholesky(running[:NC])
    factor_below = lax.linalg.triangular_solve(factor_top, running[NC:], left_side=False, lower=True, transpose_a=True)
    return (period_step, boundary, factor_top, factor_below)
```

```python
import jax
import jax.numpy as jnp
from jax import lax
from jax.experimental import pallas as pl
from jax.experimental.pallas import tpu as pltpu
from jax.sharding import PartitionSpec as P

SB = 128
HB = 128
NI = 4096
NC = 1024
NB = 2048
LOW = NI - NC
B = 128
HI = lax.Precision.HIGHEST
F32 = jnp.float32
BF16 = jnp.bfloat16
BOTH = ("period", "tile")
DEVICES = 128
CORE = 1
AXES = ((1 << 5, 3 << 5), (1 << 3, 3 << 3), (1 << 1, 3 << 1))
SHIFTS = (5, 3, 1)
TOP_COLS = ((0, 384), (384, 768), (768, 1024))


def swap(value, mask):
    return lax.ppermute(value, BOTH, [(d, d ^ mask) for d in range(DEVICES)])


def low_order(piece):
    turn, flip = piece // 2, piece % 2
    return [((turn + i) % 3, w ^ flip) for i in range(3) for w in range(2)]


def label_bit(device, axis, which):
    v = device >> SHIFTS[axis]
    return ((v ^ (v >> 1)) & 1) if which == 0 else ((v >> 1) & 1)


def low_label(device, piece):
    out = 0
    for axis, which in low_order(piece):
        out = out * 2 + label_bit(device, axis, which)
    return out


def top_label(device, axis):
    return (device & 1) * 4 + label_bit(device, axis, 0) * 2 + label_bit(device, axis, 1)


def dot_rows(a, b, **kw):
    return lax.dot_general(a, b, (((0,), (0,)), ((), ())), preferred_element_type=F32, **kw)


def dot_lanes(a, b, **kw):
    return lax.dot_general(a, b, (((1,), (1,)), ((), ())), preferred_element_type=F32, **kw)


def top_kernel(own_ref, c_ref, g_ref, send_ref, keep_ref, s_ref, acc_ref):
    for h in range(8):
        rows = slice(h * HB, (h + 1) * HB)
        s_ref[rows, :] = jnp.dot(g_ref[rows, :], c_ref[rows, :], preferred_element_type=F32).astype(BF16)
    own = [own_ref[a] for a in range(3)]
    for half in range(2):
        cols = slice(half * 512, half * 512 + 512)
        acc_ref[...] = dot_rows(c_ref[:, cols], s_ref[...])
        for jj in range(4):
            j = half * 4 + jj
            for a in range(3):
                lo, hi = TOP_COLS[a]
                where = j ^ own[a]
                spot = where & 3

                @pl.when(where >= 4)
                def _():
                    send_ref[spot, :, lo:hi] = acc_ref[jj * B:(jj + 1) * B, lo:hi]

                @pl.when(where < 4)
                def _():
                    keep_ref[spot, :, lo:hi] = acc_ref[jj * B:(jj + 1) * B, lo:hi]


def top_product(own, c, g):
    full = lambda shape: pl.BlockSpec(shape, lambda i, o: (0,) * len(shape))
    return pl.pallas_call(
        top_kernel,
        grid_spec=pltpu.PrefetchScalarGridSpec(
            num_scalar_prefetch=1,
            grid=(1,),
            in_specs=[full((1024, NC)), full((1024, HB))],
            out_specs=[full((4, B, NC)), full((4, B, NC)), full((1024, NC))],
            scratch_shapes=[pltpu.VMEM((512, NC), F32)],
        ),
        out_shape=(
            jax.ShapeDtypeStruct((4, B, NC), F32),
            jax.ShapeDtypeStruct((4, B, NC), F32),
            jax.ShapeDtypeStruct((1024, NC), BF16),
        ),
        compiler_params=pltpu.CompilerParams(vmem_limit_bytes=48 << 20),
        name="top_product",
    )(own, c, g)


def low_kernel(table_ref, core_ref, c_ref, s_ref, send_ref, keep_ref, acc_ref):
    g = pl.program_id(0)
    core = core_ref[0]
    acc_ref[...] = dot_rows(c_ref[...], s_ref[...])
    for p in range(6):
        base = table_ref[p * 8 + g]
        cols = slice((p % 2) * 512, (p % 2) * 512 + 512)
        for t in range(0, 16, 2):
            spot = p * 64 + (base ^ low_label(t, p))
            mine = pl.multiple_of(24 * (t + core) + 8 * (p // 2), 8)
            theirs = pl.multiple_of(24 * (t + 1 - core) + 8 * (p // 2), 8)
            keep_ref[spot] = acc_ref[pl.ds(mine, 8), cols]
            send_ref[spot] = acc_ref[pl.ds(theirs, 8), cols]


def low_product(table, core, c, s):
    return pl.pallas_call(
        low_kernel,
        grid_spec=pltpu.PrefetchScalarGridSpec(
            num_scalar_prefetch=2,
            grid=(8,),
            in_specs=[
                pl.BlockSpec((1024, 384), lambda i, a, b: (0, i)),
                pl.BlockSpec((1024, NC), lambda i, a, b: (0, 0)),
            ],
            out_specs=[
                pl.BlockSpec((384, 8, 512), lambda i, a, b: (0, 0, 0)),
                pl.BlockSpec((384, 8, 512), lambda i, a, b: (0, 0, 0)),
            ],
            scratch_shapes=[pltpu.VMEM((384, NC), F32)],
        ),
        out_shape=(jax.ShapeDtypeStruct((384, 8, 512), F32),) * 2,
        compiler_params=pltpu.CompilerParams(vmem_limit_bytes=52 << 20),
        name="low_product",
    )(table, core, c, s)


def storage_kernel(g_ref, link_ref, spread_ref, rhs_ref, rhs_out, part_ref, masked_ref, links_ref):
    masked_ref[...] = link_ref[...] * spread_ref[...]
    charge = jnp.zeros((8, NB), F32)
    for h in range(8):
        rows = slice(h * HB, (h + 1) * HB)
        g = g_ref[rows, :]
        m = masked_ref[rows, :]
        links_ref[rows, :] = jnp.dot(g, m, preferred_element_type=F32).astype(BF16)
        row = dot_lanes(jnp.broadcast_to(rhs_ref[h:h + 1, :], (8, HB)), g.astype(F32), precision=HI)
        rhs_out[h:h + 1, :] = row[0:1, :]
        charge = charge + jnp.dot(row.astype(BF16), m, preferred_element_type=F32)
    for k in range(NB // SB):
        cols = slice(k * SB, (k + 1) * SB)
        part_ref[k, 0:SB, :] = dot_rows(masked_ref[:, cols], links_ref[:, cols])
        part_ref[k, SB:SB + 8, :] = charge[:, cols]


def storage(g, link, spread, rhs):
    return pl.pallas_call(
        storage_kernel,
        out_shape=(
            jax.ShapeDtypeStruct((8, HB), F32),
            jax.ShapeDtypeStruct((NB // SB, SB + 8, SB), F32),
        ),
        scratch_shapes=[pltpu.VMEM((1024, NB), BF16), pltpu.VMEM((1024, NB), BF16)],
        compiler_params=pltpu.CompilerParams(vmem_limit_bytes=48 << 20),
        name="storage",
    )(g, link, spread, rhs)


def recur_kernel(own_ref, all_ref, keep_ref, out_ref, change_ref):
    own = own_ref[0]
    state = jnp.zeros((8, SB), F32)
    now = jnp.zeros((8, SB), F32)
    after = jnp.zeros((8, SB), F32)
    for s in range(8):
        spot = s ^ own
        block = all_ref[spot]
        fed = dot_lanes(state, block[0:SB, :], precision=HI)
        state = block[SB:SB + 8, :] + keep_ref[spot] * fed
        now = jnp.where(own == s, state, now)
        after = jnp.where(own + 1 == s, state, after)
    out_ref[...] = now
    change_ref[...] = now - after


def recur(own, blocks, rates):
    return pl.pallas_call(
        recur_kernel,
        in_specs=[pl.BlockSpec(memory_space=pltpu.SMEM), pl.BlockSpec(), pl.BlockSpec()],
        out_shape=(jax.ShapeDtypeStruct((8, SB), F32),) * 2,
        name="recur",
    )(own, blocks, rates)


def step_kernel(own_ref, change_ref, spread_ref, link_ref, g_ref, rhs_ref, out_ref):
    own = own_ref[0]
    pieces = [change_ref[k ^ own] for k in range(NB // SB)]
    change = jnp.concatenate(pieces, axis=1).astype(BF16) * spread_ref[...]
    linked = dot_lanes(change, link_ref[...])
    for h in range(8):
        rows = slice(h * HB, (h + 1) * HB)
        fixed = dot_lanes(linked[:, rows], g_ref[rows, :].astype(F32), precision=HI)
        out_ref[h:h + 1, :] = rhs_ref[h:h + 1, :] - fixed[0:1, :]


def step(own, change, spread, link, g, solved):
    return pl.pallas_call(
        step_kernel,
        in_specs=[pl.BlockSpec(memory_space=pltpu.SMEM)] + [pl.BlockSpec()] * 5,
        out_shape=jax.ShapeDtypeStruct((8, HB), F32),
        compiler_params=pltpu.CompilerParams(vmem_limit_bytes=32 << 20),
        name="step",
    )(own, change, spread, link, g, solved)


def eliminate(d_ref):
    sub = lax.broadcasted_iota(jnp.int32, (8, B), 0)

    def sb(v, t):
        return jnp.broadcast_to(v[t:t + 1, :], (8, B))

    for p in range(B // 8):
        here = slice(8 * p, 8 * p + 8)
        v0 = d_ref[here, 0:B]
        v1 = d_ref[here, B:2 * B]
        cols = [jnp.broadcast_to(v0[:, 8 * p + t:8 * p + t + 1], (8, B)) for t in range(8)]
        u0 = v0
        u1 = v1
        for t in range(8):
            r = lax.rsqrt(sb(cols[t], t))
            inv = r * r
            row0 = sb(v0, t)
            row1 = sb(v1, t)
            at = sub == t
            u0 = jnp.where(at, row0 * r, u0)
            u1 = jnp.where(at, row1 * r, u1)
            row0 = row0 * inv
            row1 = row1 * inv
            for q in range(t + 1, 8):
                rc = sb(cols[q], t) * inv
                cols[q] = jnp.where(at, rc, cols[q] - cols[t] * rc)
            v0 = jnp.where(at, row0, v0 - cols[t] * row0)
            v1 = jnp.where(at, row1, v1 - cols[t] * row1)
        d_ref[here, 0:B] = u0
        d_ref[here, B:2 * B] = u1
        z0 = [sb(v0, t) for t in range(8)]
        z1 = [sb(v1, t) for t in range(8)]
        for q in range(p + 1, B // 8):
            there = slice(8 * q, 8 * q + 8)
            old = d_ref[there, 0:B]
            r0 = old
            r1 = d_ref[there, B:2 * B]
            for t in range(8):
                m = jnp.broadcast_to(old[:, 8 * p + t:8 * p + t + 1], (8, B))
                r0 = r0 - m * z0[t]
                r1 = r1 - m * z1[t]
            d_ref[there, 0:B] = r0
            d_ref[there, B:2 * B] = r1


def chol_kernel(own_ref, mine_a, theirs_a, mine_b, theirs_b, mine_c, theirs_c, diag_ref, l_ref, w_ref, s_ref, d_ref):
    rows = lax.broadcasted_iota(jnp.int32, (B, B), 0)
    lanes = lax.broadcasted_iota(jnp.int32, (B, B), 1)
    eye = (rows == lanes).astype(F32)
    wide = lax.broadcasted_iota(jnp.int32, (B, NC), 1)
    deep = lax.broadcasted_iota(jnp.int32, (B, NC), 0)
    halves = ((mine_a, theirs_a), (mine_b, theirs_b), (mine_c, theirs_c))
    for a in range(3):
        lo, hi = TOP_COLS[a]
        own = own_ref[a]
        for r in range(8):
            spot = pl.multiple_of((r ^ own) * B, B)
            s_ref[pl.ds(spot, B), lo:hi] = halves[a][r // 4][r % 4]

    def panel(k, carry):
        base = pl.multiple_of(k * B, B)
        here = pl.ds(base, B)
        d_ref[:, 0:B] = s_ref[here, here] + jnp.where(rows == lanes, diag_ref[:, here], 0.0)
        d_ref[:, B:2 * B] = eye
        eliminate(d_ref)
        w = d_ref[:, B:2 * B]
        w_ref[here, :] = w
        strip = jnp.dot(w, s_ref[here, :], precision=HI, preferred_element_type=F32)
        strip = jnp.where(wide >= base + deep, strip, 0.0)
        s_ref[here, :] = strip
        s_ref[here, here] = jnp.where(lanes >= rows, d_ref[:, 0:B], 0.0)

        def trail(i, c):
            there = pl.ds(pl.multiple_of(i * B, B), B)
            left = s_ref[here, there]
            s_ref[there, :] -= dot_rows(left, s_ref[here, :], precision=HI)
            return c

        lax.fori_loop(k + 1, NC // B, trail, 0)
        for j in range(NC // B):
            l_ref[j * B:(j + 1) * B, here] = s_ref[here, j * B:(j + 1) * B].T
        return carry

    lax.fori_loop(0, NC // B, panel, 0)


def chol(own, parts, diag):
    return pl.pallas_call(
        chol_kernel,
        in_specs=[pl.BlockSpec(memory_space=pltpu.SMEM)] + [pl.BlockSpec()] * 7,
        out_shape=(jax.ShapeDtypeStruct((NC, NC), F32), jax.ShapeDtypeStruct((NC, B), F32)),
        scratch_shapes=[pltpu.VMEM((NC, NC), F32), pltpu.VMEM((B, 2 * B), F32)],
        compiler_params=pltpu.CompilerParams(vmem_limit_bytes=48 << 20),
        name="chol",
    )(own, *parts, diag)


def below_kernel(b_ref, l_ref, w_ref, x_ref, r_ref):
    r_ref[...] = b_ref[...]
    for k in range(NC // B):
        here = slice(k * B, (k + 1) * B)
        x = dot_lanes(r_ref[:, here], w_ref[here, :], precision=HI)
        x_ref[:, here] = x
        if k + 1 < NC // B:
            rest = slice((k + 1) * B, NC)
            r_ref[:, rest] -= dot_lanes(x, l_ref[rest, here], precision=HI)


def below(b, l, w):
    rows = b.shape[0]
    return pl.pallas_call(
        below_kernel,
        out_shape=jax.ShapeDtypeStruct((rows, NC), F32),
        scratch_shapes=[pltpu.VMEM((rows, NC), F32)],
        compiler_params=pltpu.CompilerParams(vmem_limit_bytes=32 << 20),
        name="below",
    )(b, l, w)


def pick(value, axis, index):
    return lax.dynamic_index_in_dim(value, index, axis, keepdims=False)


def boundary_terms(part, rate, period, tile):
    core, z0, z1, ylo = tile & 1, (tile >> 1) & 1, (tile >> 2) & 1, (tile >> 3) & 1
    v = part.reshape(2, 2, 2, 2, SB + 8, SB)
    for axis, bit, mask in ((3, core, 1), (2, z0, 2), (0, ylo, 8), (0, z1, 4)):
        v = pick(v, axis, bit) + swap(pick(v, axis, 1 - bit), mask)
    v = jnp.concatenate([v, jnp.broadcast_to(rate, (8, SB))], axis=0)[None]
    for mask in (16, 32, 64):
        v = jnp.concatenate([v, swap(v, mask)], axis=0)
    return v


def shards(block_inv, linking, block_mask, period_rhs, retention, invest_cols, invest_diag):
    g = block_inv[0]
    link = linking[0]
    c = invest_cols[0]
    period = lax.axis_index("period").astype(jnp.int32)
    tile = lax.axis_index("tile").astype(jnp.int32)
    me = period * 16 + tile
    core = me & 1
    top_own = jnp.stack([top_label(me, a) for a in range(3)])
    table = jnp.stack([low_label(gg * 16, p) ^ low_label(me, p) for p in range(6) for gg in range(8)])

    send, keep, scaled = top_product(top_own, c[:, :NC], g)
    both = keep + swap(send, CORE)
    tops = []
    for a in range(3):
        lo, hi = TOP_COLS[a]
        v = both[:, :, lo:hi]
        for mask in AXES[a]:
            half = v.shape[0] // 2
            v = v[:half] + swap(v[half:], mask)
        tops.append(v)
    for turn in (1, 2):
        for w in range(2):
            tops = [v + swap(v, AXES[(a + turn) % 3][w]) for a, v in enumerate(tops)]
    for w in (1, 0):
        tops = [jnp.concatenate([v, swap(v, AXES[a][w])], axis=0) for a, v in enumerate(tops)]
    parts = []
    for v in tops:
        parts += [v, swap(v, CORE)]

    low_send, low_keep = low_product(table, core[None], c[:, NC:], scaled)
    low = low_keep + swap(low_send, CORE)

    spread = jnp.repeat(block_mask[0], SB).astype(BF16)[None, :]
    solved, part = storage(g, link, spread, period_rhs.reshape(8, HB))
    gathered = boundary_terms(part, retention, period, tile)
    carried8, change8 = recur(period[None], gathered[:, :SB + 8], gathered[:, SB + 8:])
    v = change8[None]
    for mask in (1, 2, 4, 8):
        v = jnp.concatenate([v, swap(v, mask)], axis=0)
    period_step = step(tile[None], v, spread, link, g, solved).reshape(1, 1024)

    low, parts = lax.optimization_barrier((low, parts))
    factor_top, inverses = chol(top_own, parts, invest_diag[None, :])
    pieces = [low[64 * p:64 * p + 64] for p in range(6)]
    for i in range(6):
        nxt = []
        for p in range(6):
            axis, which = low_order(p)[i]
            half = pieces[p].shape[0] // 2
            nxt.append(pieces[p][:half] + swap(pieces[p][half:], AXES[axis][which]))
        pieces = nxt
    pieces = [v[0] for v in pieces]
    rows = [jnp.concatenate([pieces[2 * a], pieces[2 * a + 1]], axis=1) for a in range(3)]
    factor_below = below(jnp.concatenate(rows, axis=0), factor_top, inverses)
    return (period_step, carried8[0:1], factor_top, factor_below)


def solution(mesh):
    placed = (
        P("period", "tile", None),
        P("period", "tile", None),
        P("period", None),
        P("period", "tile"),
        P("period", "tile"),
        P("period", "tile", None),
        P(),
    )
    return jax.shard_map(
        shards,
        mesh=mesh,
        in_specs=placed,
        out_specs=(P("period", "tile"), P("period", "tile"), P(), P(("period", "tile"), None)),
        check_vma=False,
    )
```

```python
import jax
import jax.numpy as jnp
from jax import lax
from jax.experimental import pallas as pl
from jax.experimental.pallas import tpu as pltpu
from jax.sharding import PartitionSpec as P

SB = 128
HB = 128
NI = 4096
NC = 1024
NB = 2048
LOW = NI - NC
B = 128
HI = lax.Precision.HIGHEST
F32 = jnp.float32
BF16 = jnp.bfloat16
BOTH = ("period", "tile")
DEVICES = 128
CORE = 1
AXES = ((1 << 5, 3 << 5), (1 << 3, 3 << 3), (1 << 1, 3 << 1))
SHIFTS = (5, 3, 1)
WIDE = 384
HALF = NC // 2


def swap(value, mask):
    return lax.ppermute(value, BOTH, [(d, d ^ mask) for d in range(DEVICES)])


def low_order(piece):
    turn, flip = piece // 2, piece % 2
    first = [(turn, flip), (turn, 1 - flip)]
    return first + [((turn + i) % 3, w) for i in (1, 2) for w in range(2)]


def label_bit(device, axis, which):
    v = device >> SHIFTS[axis]
    return ((v ^ (v >> 1)) & 1) if which == 0 else ((v >> 1) & 1)


def low_label(device, piece):
    out = 0
    for axis, which in low_order(piece):
        out = out * 2 + label_bit(device, axis, which)
    return out


def top_label(device, axis):
    return (device & 1) * 4 + label_bit(device, axis, 0) * 2 + label_bit(device, axis, 1)


def dot_rows(a, b, **kw):
    return lax.dot_general(a, b, (((0,), (0,)), ((), ())), preferred_element_type=F32, **kw)


def dot_lanes(a, b, **kw):
    return lax.dot_general(a, b, (((1,), (1,)), ((), ())), preferred_element_type=F32, **kw)


def spot_of(unit, q):
    i = unit >> 1
    first = q < 8 - i
    row = jnp.where(first, i, 7 - i) * B + (unit & 1) * 64
    col = jnp.where(first, i + q, q - 1) * B
    return pl.ds(pl.multiple_of(row, 64), 64), pl.ds(pl.multiple_of(col, B), B)


def top_kernel(own_ref, c_ref, g_ref, send_ref, keep_ref, s_ref, acc_ref):
    for h in range(8):
        rows = slice(h * HB, (h + 1) * HB)
        s_ref[rows, :] = jnp.dot(g_ref[rows, :], c_ref[rows, :], preferred_element_type=F32).astype(BF16)
    acc_ref[0:HALF, :] = dot_rows(c_ref[:, 0:HALF], s_ref[...])
    acc_ref[HALF:NC, HALF:NC] = dot_rows(c_ref[:, HALF:NC], s_ref[:, HALF:NC])
    for q in range(9):
        own = own_ref[q // 3]
        for r in range(8):
            rows, cols = spot_of(r ^ own, q)
            out = keep_ref if r < 4 else send_ref
            out[r % 4, :, q * B:(q + 1) * B] = acc_ref[rows, cols]


def top_product(own, c, g):
    full = lambda shape: pl.BlockSpec(shape, lambda i, o: (0,) * len(shape))
    return pl.pallas_call(
        top_kernel,
        grid_spec=pltpu.PrefetchScalarGridSpec(
            num_scalar_prefetch=1,
            grid=(1,),
            in_specs=[full((1024, NC)), full((1024, HB))],
            out_specs=[full((4, 64, 3 * WIDE)), full((4, 64, 3 * WIDE)), full((1024, NC))],
            scratch_shapes=[pltpu.VMEM((NC, NC), F32)],
        ),
        out_shape=(
            jax.ShapeDtypeStruct((4, 64, 3 * WIDE), F32),
            jax.ShapeDtypeStruct((4, 64, 3 * WIDE), F32),
            jax.ShapeDtypeStruct((1024, NC), BF16),
        ),
        compiler_params=pltpu.CompilerParams(vmem_limit_bytes=48 << 20),
        name="top_product",
    )(own, c, g)


def low_kernel(table_ref, core_ref, c_ref, s_ref, send_ref, keep_ref, acc_ref):
    core = core_ref[0]
    acc_ref[...] = dot_rows(c_ref[...], s_ref[...])
    for gg in range(2):
        g = pl.program_id(0) * 2 + gg
        for p in range(6):
            base = table_ref[p * 8 + g]
            cols = slice((p % 2) * 512, (p % 2) * 512 + 512)
            for t in range(0, 16, 2):
                spot = p * 64 + (base ^ low_label(t, p))
                mine = pl.multiple_of(384 * gg + 24 * (t + core) + 8 * (p // 2), 8)
                theirs = pl.multiple_of(384 * gg + 24 * (t + 1 - core) + 8 * (p // 2), 8)
                keep_ref[spot] = acc_ref[pl.ds(mine, 8), cols]
                send_ref[spot] = acc_ref[pl.ds(theirs, 8), cols]


def low_product(table, core, c, s):
    return pl.pallas_call(
        low_kernel,
        grid_spec=pltpu.PrefetchScalarGridSpec(
            num_scalar_prefetch=2,
            grid=(4,),
            in_specs=[
                pl.BlockSpec((pl.Element(1024), pl.Element(768)), lambda i, a, b: (0, pl.multiple_of(NC + 768 * i, B))),
                pl.BlockSpec((1024, NC), lambda i, a, b: (0, 0)),
            ],
            out_specs=[
                pl.BlockSpec((384, 8, 512), lambda i, a, b: (0, 0, 0)),
                pl.BlockSpec((384, 8, 512), lambda i, a, b: (0, 0, 0)),
            ],
            scratch_shapes=[pltpu.VMEM((768, NC), F32)],
        ),
        out_shape=(jax.ShapeDtypeStruct((384, 8, 512), F32),) * 2,
        compiler_params=pltpu.CompilerParams(vmem_limit_bytes=56 << 20),
        name="low_product",
    )(table, core, c, s)


def storage_kernel(g_ref, link_ref, spread_ref, rhs_ref, rhs_out, part_ref, masked_ref, links_ref):
    masked_ref[...] = link_ref[...] * spread_ref[...]
    charge = jnp.zeros((8, NB), F32)
    for h in range(8):
        rows = slice(h * HB, (h + 1) * HB)
        g = g_ref[rows, :]
        m = masked_ref[rows, :]
        links_ref[rows, :] = jnp.dot(g, m, preferred_element_type=F32).astype(BF16)
        row = dot_lanes(jnp.broadcast_to(rhs_ref[h:h + 1, :], (8, HB)), g.astype(F32), precision=HI)
        rhs_out[h:h + 1, :] = row[0:1, :]
        charge = charge + jnp.dot(row.astype(BF16), m, preferred_element_type=F32)
    for k in range(NB // SB):
        cols = slice(k * SB, (k + 1) * SB)
        part_ref[k, 0:SB, :] = dot_rows(masked_ref[:, cols], links_ref[:, cols])
        part_ref[k, SB:SB + 8, :] = charge[:, cols]


def storage(g, link, spread, rhs):
    return pl.pallas_call(
        storage_kernel,
        out_shape=(
            jax.ShapeDtypeStruct((8, HB), F32),
            jax.ShapeDtypeStruct((NB // SB, SB + 8, SB), F32),
        ),
        scratch_shapes=[pltpu.VMEM((1024, NB), BF16), pltpu.VMEM((1024, NB), BF16)],
        compiler_params=pltpu.CompilerParams(vmem_limit_bytes=48 << 20),
        name="storage",
    )(g, link, spread, rhs)


def recur_kernel(own_ref, all_ref, out_ref, change_ref):
    own = own_ref[0]
    state = jnp.zeros((8, SB), F32)
    now = jnp.zeros((8, SB), F32)
    after = jnp.zeros((8, SB), F32)
    for s in range(8):
        spot = s ^ own
        block = all_ref[spot]
        fed = dot_lanes(state, block[0:SB, :], precision=HI)
        state = block[SB:SB + 8, :] + block[SB + 8:SB + 16, :] * fed
        now = jnp.where(own == s, state, now)
        after = jnp.where(own + 1 == s, state, after)
    out_ref[...] = now
    change_ref[...] = now - after


def recur(own, blocks):
    return pl.pallas_call(
        recur_kernel,
        in_specs=[pl.BlockSpec(memory_space=pltpu.SMEM), pl.BlockSpec()],
        out_shape=(jax.ShapeDtypeStruct((8, SB), F32),) * 2,
        name="recur",
    )(own, blocks)


def step_kernel(own_ref, change_ref, spread_ref, link_ref, g_ref, rhs_ref, out_ref):
    own = own_ref[0]
    pieces = [change_ref[k ^ own] for k in range(NB // SB)]
    change = jnp.concatenate(pieces, axis=1).astype(BF16) * spread_ref[...]
    linked = dot_lanes(change, link_ref[...])
    for h in range(8):
        rows = slice(h * HB, (h + 1) * HB)
        fixed = dot_lanes(linked[:, rows], g_ref[rows, :].astype(F32), precision=HI)
        out_ref[h:h + 1, :] = rhs_ref[h:h + 1, :] - fixed[0:1, :]


def step(own, change, spread, link, g, solved):
    return pl.pallas_call(
        step_kernel,
        in_specs=[pl.BlockSpec(memory_space=pltpu.SMEM)] + [pl.BlockSpec()] * 5,
        out_shape=jax.ShapeDtypeStruct((8, HB), F32),
        compiler_params=pltpu.CompilerParams(vmem_limit_bytes=32 << 20),
        name="step",
    )(own, change, spread, link, g, solved)


def eliminate(d_ref, fillers):
    sub = lax.broadcasted_iota(jnp.int32, (8, B), 0)
    def sb(v, t):
        return jnp.broadcast_to(v[t:t + 1, :], (8, B))
    at = [sub == t for t in range(8)]
    for p in range(B // 8):
        here = slice(8 * p, 8 * p + 8)
        v0 = d_ref[here, 0:B]
        v1 = d_ref[here, B:2 * B]
        cols = [jnp.broadcast_to(v0[:, 8 * p + t:8 * p + t + 1], (8, B)) for t in range(8)]
        u0 = v0
        u1 = v1
        for t in range(0, 8, 2):
            ca, cb = cols[t], cols[t + 1]
            a, b, d = sb(ca, t), sb(ca, t + 1), sb(cb, t + 1)
            det = a * d - b * b
            r = lax.rsqrt(det)
            inv = r * r
            ia, ib, id_ = a * inv, b * inv, d * inv
            ra = lax.rsqrt(a)
            under = b * (ra * ra)
            rd = r * (a * ra)

            def fold(x):
                xt, xu = sb(x, t), sb(x, t + 1)
                zt = id_ * xt - ib * xu
                zu = ia * xu - ib * xt
                rest = x - (ca * zt + cb * zu)
                return xt, xu, jnp.where(at[t], zt, jnp.where(at[t + 1], zu, rest))

            for q in range(t + 2, 8):
                cols[q] = fold(cols[q])[2]
            xt, xu, v0 = fold(v0)
            u0 = jnp.where(at[t], xt * ra, jnp.where(at[t + 1], (xu - under * xt) * rd, u0))
            xt, xu, v1 = fold(v1)
            u1 = jnp.where(at[t], xt * ra, jnp.where(at[t + 1], (xu - under * xt) * rd, u1))
        d_ref[here, 0:B] = u0
        d_ref[here, B:2 * B] = u1
        if p < len(fillers):
            fillers[p]()
        z0 = [sb(v0, t) for t in range(8)]
        z1 = [sb(v1, t) for t in range(8)]
        for q in range(p + 1, B // 8):
            there = slice(8 * q, 8 * q + 8)
            old = d_ref[there, 0:B]
            m = [jnp.broadcast_to(old[:, 8 * p + t:8 * p + t + 1], (8, B)) for t in range(8)]
            s0 = [m[t] * z0[t] for t in range(8)]
            s1 = [m[t] * z1[t] for t in range(8)]
            tree = lambda s: ((s[0] + s[1]) + (s[2] + s[3])) + ((s[4] + s[5]) + (s[6] + s[7]))
            d_ref[there, 0:B] = old - tree(s0)
            d_ref[there, B:2 * B] = d_ref[there, B:2 * B] - tree(s1)


def split(x):
    hi = x.astype(BF16)
    return hi, (x - hi.astype(F32)).astype(BF16)


def chol_kernel(own_ref, mine_a, theirs_a, mine_b, theirs_b, mine_c, theirs_c, diag_ref, low_ref, l_ref, x_ref,
                s_ref, d_ref, lhs_ref, rhs_ref, r_ref, xs_ref):
    rows = lax.broadcasted_iota(jnp.int32, (B, B), 0)
    lanes = lax.broadcasted_iota(jnp.int32, (B, B), 1)
    eye = (rows == lanes).astype(F32)
    halves = ((mine_a, theirs_a), (mine_b, theirs_b), (mine_c, theirs_c))
    for q in range(9):
        own = own_ref[q // 3]
        for r in range(8):
            where = spot_of(r ^ own, q)
            s_ref[where] = halves[q // 3][r // 4][r % 4, :, (q % 3) * B:(q % 3 + 1) * B]
    l_ref[...] = jnp.zeros((NC, NC), F32)
    lhs_ref[...] = jnp.zeros((NC, 3 * B), BF16)
    rhs_ref[...] = jnp.zeros((3 * B, NC), BF16)
    r_ref[...] = low_ref[...]
    xs_ref[...] = jnp.zeros(xs_ref.shape, BF16)

    def update(there, cols):
        s_ref[there, cols] -= jnp.dot(lhs_ref[there, :], rhs_ref[:, cols], preferred_element_type=F32)

    def update_low():
        r_ref[...] -= jnp.dot(xs_ref[...], rhs_ref[...], preferred_element_type=F32)

    fillers = [update_low]
    for i in range(1, 8):
        there = slice(i * B, (i + 1) * B)
        if i < 4:
            fillers.append(lambda there=there: update(there, slice(0, HALF)))
        fillers.append(lambda there=there: update(there, slice(HALF, NC)))

    def panel(k, carry):
        here = pl.ds(pl.multiple_of(k * B, B), B)
        update(here, slice(0, NC))
        lhs_ref[here, :] = jnp.zeros((B, 3 * B), BF16)
        d_ref[:, 0:B] = s_ref[here, here] + jnp.where(rows == lanes, diag_ref[:, here], 0.0)
        d_ref[:, B:2 * B] = eye
        eliminate(d_ref, fillers)
        l_ref[here, here] = jnp.where(lanes >= rows, d_ref[:, 0:B], 0.0).T
        wh, wl = split(d_ref[:, B:2 * B])
        w3 = jnp.concatenate([wh, wh, wl], axis=1)
        rh, rl = split(r_ref[:, here])
        x = dot_lanes(jnp.concatenate([rh, rl, rh], axis=1), w3)
        x_ref[:, here] = x
        xh, xl = split(x)
        xs_ref[...] = jnp.concatenate([xh, xh, xl], axis=1)

        def strip(lo):
            cols = slice(lo, lo + HALF)
            ah, al = split(s_ref[here, cols])
            y = jnp.dot(w3, jnp.concatenate([ah, al, ah], axis=0), preferred_element_type=F32)
            yh, yl = split(y)
            rhs_ref[0:B, cols] = yh
            rhs_ref[B:2 * B, cols] = yl
            rhs_ref[2 * B:3 * B, cols] = yh
            for j in range(lo // B, (lo + HALF) // B):
                @pl.when(j > k)
                def _():
                    t = y[:, j * B - lo:(j + 1) * B - lo].T
                    l_ref[j * B:(j + 1) * B, here] = t
                    th, tl = split(t)
                    lhs_ref[j * B:(j + 1) * B, 0:B] = th
                    lhs_ref[j * B:(j + 1) * B, B:2 * B] = th
                    lhs_ref[j * B:(j + 1) * B, 2 * B:3 * B] = tl

        @pl.when(k < 3)
        def _():
            strip(0)

        @pl.when(k < 7)
        def _():
            strip(HALF)

        return carry

    lax.fori_loop(0, NC // B, panel, 0)


def chol(own, parts, diag, low):
    rows = low.shape[0]
    return pl.pallas_call(
        chol_kernel,
        in_specs=[pl.BlockSpec(memory_space=pltpu.SMEM)] + [pl.BlockSpec()] * 8,
        out_shape=(jax.ShapeDtypeStruct((NC, NC), F32), jax.ShapeDtypeStruct((rows, NC), F32)),
        scratch_shapes=[
            pltpu.VMEM((NC, NC), F32),
            pltpu.VMEM((B, 2 * B), F32),
            pltpu.VMEM((NC, 3 * B), BF16),
            pltpu.VMEM((3 * B, NC), BF16),
            pltpu.VMEM((rows, NC), F32),
            pltpu.VMEM((rows, 3 * B), BF16),
        ],
        compiler_params=pltpu.CompilerParams(vmem_limit_bytes=48 << 20),
        name="chol",
    )(own, *parts, diag, low)


def pick(value, axis, index):
    return lax.dynamic_index_in_dim(value, index, axis, keepdims=False)


def boundary_terms(part, rate, period, tile):
    core, z0, z1, ylo = tile & 1, (tile >> 1) & 1, (tile >> 2) & 1, (tile >> 3) & 1
    v = part.reshape(2, 2, 2, 2, SB + 8, SB)
    for axis, bit, mask in ((3, core, 1), (2, z0, 2), (0, ylo, 8), (0, z1, 4)):
        v = pick(v, axis, bit) + swap(pick(v, axis, 1 - bit), mask)
    v = jnp.concatenate([v, jnp.broadcast_to(rate, (8, SB))], axis=0)[None]
    for mask in (16, 32, 64):
        v = jnp.concatenate([v, swap(v, mask)], axis=0)
    return v


def shards(block_inv, linking, block_mask, period_rhs, retention, invest_cols, invest_diag):
    g = block_inv[0]
    link = linking[0]
    c = invest_cols[0]
    period = lax.axis_index("period").astype(jnp.int32)
    tile = lax.axis_index("tile").astype(jnp.int32)
    me = period * 16 + tile
    core = me & 1
    top_own = jnp.stack([top_label(me, a) for a in range(3)])
    table = jnp.stack([low_label(gg * 16, p) ^ low_label(me, p) for p in range(6) for gg in range(8)])

    send, keep, scaled = top_product(top_own, c, g)
    both = keep + swap(send, CORE)
    tops = []
    for a in range(3):
        v = both[:, :, a * WIDE:(a + 1) * WIDE]
        for mask in AXES[a]:
            half = v.shape[0] // 2
            v = v[:half] + swap(v[half:], mask)
        tops.append(v)
    for turn in (1, 2):
        for w in range(2):
            tops = [v + swap(v, AXES[(a + turn) % 3][w]) for a, v in enumerate(tops)]
    for w in (1, 0):
        tops = [jnp.concatenate([v, swap(v, AXES[a][w])], axis=0) for a, v in enumerate(tops)]
    parts = []
    for v in tops:
        parts += [v, swap(v, CORE)]

    low_send, low_keep = low_product(table, core[None], c, scaled)
    low = low_keep + swap(low_send, CORE)
    pieces = [low[64 * p:64 * p + 64] for p in range(6)]

    def halve(values, i, step_of):
        out = []
        for p, v in enumerate(values):
            axis, which = low_order(step_of * p)[i]
            half = v.shape[0] // 2
            out.append(v[:half] + swap(v[half:], AXES[axis][which]))
        return out

    for i in range(2):
        pieces = halve(pieces, i, 1)
    pieces = [jnp.concatenate([pieces[2 * a], pieces[2 * a + 1]], axis=2) for a in range(3)]
    for i in range(2, 6):
        pieces = halve(pieces, i, 2)
    own_low = jnp.concatenate([v[0] for v in pieces], axis=0)

    spread = jnp.repeat(block_mask[0], SB).astype(BF16)[None, :]
    solved, part = storage(g, link, spread, period_rhs.reshape(8, HB))
    gathered = boundary_terms(part, retention, period, tile)
    carried8, change8 = recur(period[None], gathered)
    v = change8[None]
    for mask in (1, 2, 4, 8):
        v = jnp.concatenate([v, swap(v, mask)], axis=0)
    period_step = step(tile[None], v, spread, link, g, solved).reshape(1, 1024)

    factor_top, factor_below = chol(top_own, parts, invest_diag[None, :], own_low)
    return (period_step, carried8[0:1], factor_top, factor_below)


def solution(mesh):
    placed = (
        P("period", "tile", None),
        P("period", "tile", None),
        P("period", None),
        P("period", "tile"),
        P("period", "tile"),
        P("period", "tile", None),
        P(),
    )
    return jax.shard_map(
        shards,
        mesh=mesh,
        in_specs=placed,
        out_specs=(P("period", "tile"), P("period", "tile"), P(), P(("period", "tile"), None)),
        check_vma=False,
    )
```
